32 devices in a mesh: doc: 4 (over y, x), cen: 8 (over z, core).
Axes of the slice: x: 2, y: 2, z: 4, core: 2. Of those that a mesh axis runs over, the one named last changes fastest.
Arguments:
- passages: bfloat16 [1536, 1024], P(('doc', 'cen')), may hold values from -64 to 64
- centroids: bfloat16 [8192, 1024], P('cen'), may hold values from -64 to 64
Outputs:
- assign: bfloat16 [1536, 8192], P('doc', 'cen')
- masses: float32 [8192], P('cen')
- new_centroids: float32 [8192, 1024], P('cen', 'doc')
The draws below stay inside these ranges and needn't reach their ends.
All inputs are finite; a program needn't handle non-finite values.
Results may differ from the reference program's by a relative error of at most 0.008.
Values may be sent and summed in bfloat16 or wider, within the bound.
A program may use at most 64 MiB of HBM per device.

```python
import math
import jax
import jax.numpy as jnp
from jax import lax

D = 1024
ITERS = 3
CENTROIDS = 8192
N_ROWS = 1536
N_DOC = 4


def shared_draw(key):
    first_key = jax.random.fold_in(key, 11)
    second_key = jax.random.fold_in(key, 12)
    rows_raw = jax.random.normal(first_key, (N_ROWS, D), jnp.float32)
    cols_raw = jax.random.normal(second_key, (CENTROIDS, D), jnp.float32)
    row_scale = jnp.exp(jax.random.uniform(jax.random.fold_in(key, 13), (N_ROWS, 1), jnp.float32, math.log(0.3), math.log(3.0)))
    col_scale = jnp.exp(jax.random.uniform(jax.random.fold_in(key, 14), (CENTROIDS, 1), jnp.float32, math.log(0.3), math.log(3.0)))
    rows_out = rows_raw * row_scale
    cols_out = cols_raw * col_scale
    return (jnp.clip(rows_out, -64.0, 64.0), jnp.clip(cols_out, -64.0, 64.0))


def draw_passages(key, part):
    return shared_draw(key)[0].astype(jnp.bfloat16)


def draw_centroids(key, part):
    return shared_draw(key)[1].astype(jnp.bfloat16)


def setup_inputs(seed: int = 0) -> dict:
    arg_keys = jax.random.split(jax.random.key(seed), 3)
    return {
        "passages": draw_passages(jax.random.fold_in(arg_keys[2], 71), 0),
        "centroids": draw_centroids(jax.random.fold_in(arg_keys[2], 71), 0),
    }


def reference(passages, centroids):
    scale = 1.0 / math.sqrt(D)
    scores = lax.dot_general(passages, centroids, (((1,), (1,)), ((), ())), preferred_element_type=jnp.float32) * scale
    log_column = math.log(N_ROWS / CENTROIDS)
    col_potential = jnp.zeros((CENTROIDS,), jnp.float32)
    for iteration in range(ITERS):
        row_potential = -jax.nn.logsumexp(scores + col_potential[None, :], axis=1)
        col_potential = log_column - jax.nn.logsumexp(scores + row_potential[:, None], axis=0)
    row_potential = -jax.nn.logsumexp(scores + col_potential[None, :], axis=1)
    weights = jnp.exp(scores + row_potential[:, None] + col_potential[None, :])
    assign = (weights * CENTROIDS).astype(jnp.bfloat16)
    raw_mass = lax.optimization_barrier(jnp.sum(weights, axis=0))
    grouped_assign = assign.reshape(N_DOC, N_ROWS // N_DOC, CENTROIDS)
    grouped_rows = passages.reshape(N_DOC, N_ROWS // N_DOC, D)

    def accumulate(total, pair):
        partial_value = lax.dot_general(pair[0], pair[1], (((0,), (0,)), ((), ())), preferred_element_type=jnp.float32)
        rounded = lax.optimization_barrier(partial_value.astype(jnp.bfloat16))
        return (total + rounded.astype(jnp.float32), 0)
    sums, unused = lax.scan(accumulate, jnp.zeros((CENTROIDS, D), jnp.float32), (grouped_assign, grouped_rows))
    new_centroids = sums / CENTROIDS / raw_mass[:, None]
    masses = raw_mass * CENTROIDS / N_ROWS
    return (assign, masses, new_centroids)
```

```python
import functools
import math

import jax
import jax.numpy as jnp
from jax import lax
from jax.experimental import pallas as pl
from jax.experimental.pallas import tpu as pltpu
from jax.sharding import PartitionSpec as P

ITERS = 3
MESH = pl.DeviceIdType.MESH
LANES = 128


def kernel(
    nd, nc, p_ref, c_ref, assign_out, mass_out, newc_out,
    rows_v, cent_v, scores, rp_v, tbuf, row_slots, col_slots, mass_slots, assign_v, part_send, part_recv, newc_v,
    load_sem, gs_sem, gr_sem, rs_sem, rr_sem, cs_sem, cr_sem, ms_sem, mr_sem, ps_sem, pr_sem, out_sem,
):
    d = lax.axis_index("doc")
    c = lax.axis_index("cen")
    block, width = p_ref.shape
    cols = c_ref.shape[0]
    rows = nc * block
    feats = width // nd
    total_cols = cols * nc
    total_rows = rows * nd
    scale = 1.0 / math.sqrt(width)
    log_column = math.log(total_rows / total_cols)
    sends = []

    load_p = pltpu.make_async_copy(p_ref, rows_v.at[c], load_sem.at[0])
    load_c = pltpu.make_async_copy(c_ref, cent_v, load_sem.at[1])
    load_p.start()
    load_c.start()

    barrier = pltpu.get_barrier_semaphore()
    for k in range(1, nc):
        pl.semaphore_signal(barrier, inc=1, device_id=(d, lax.rem(c + k, nc)), device_id_type=MESH)
    for k in range(1, nd):
        pl.semaphore_signal(barrier, inc=1, device_id=(lax.rem(d + k, nd), c), device_id_type=MESH)
    pl.semaphore_wait(barrier, nc + nd - 2)
    load_p.wait()

    def push(src, dst, send, recv, where):
        copy = pltpu.make_async_remote_copy(
            src_ref=src, dst_ref=dst, send_sem=send, recv_sem=recv, device_id=where, device_id_type=MESH
        )
        copy.start()
        sends.append(copy)

    def arrive(ref, send, recv):
        pltpu.make_async_remote_copy(
            src_ref=ref, dst_ref=ref, send_sem=send, recv_sem=recv, device_id=(d, c), device_id_type=MESH
        ).wait_recv()

    mate = c + 1 - 2 * lax.rem(c, 2)
    half = nc // 2
    for k in range(1, half):
        push(rows_v.at[c], rows_v.at[c], gs_sem.at[k], gr_sem.at[c], (d, lax.rem(c + 2 * k, nc)))
    push(rows_v.at[c], rows_v.at[c], gs_sem.at[0], gr_sem.at[c], (d, mate))
    order = [k for pair in zip(range(1, half), reversed(range(1, half))) for k in pair][: half - 1]
    for k in order:
        src = lax.rem(c + nc - 2 * k, nc)
        arrive(rows_v.at[src], gs_sem.at[half + k], gr_sem.at[src])
        push(rows_v.at[src], rows_v.at[src], gs_sem.at[half + k], gr_sem.at[src], (d, mate))
    arrive(rows_v.at[mate], gs_sem.at[0], gr_sem.at[mate])
    for k in range(1, half):
        src = lax.rem(mate + nc - 2 * k, nc)
        arrive(rows_v.at[src], gs_sem.at[0], gr_sem.at[src])
    load_c.wait()

    group_rows = rows_v[...].reshape(rows, width)
    tile = min(256, cols)
    for j in range(cols // tile):
        at = slice(j * tile, (j + 1) * tile)
        scores[:, at] = (
            lax.dot_general(
                group_rows, cent_v[at, :], (((1,), (1,)), ((), ())), preferred_element_type=jnp.float32
            )
            * scale
        )

    step_rows = 64
    lane = lax.broadcasted_iota(jnp.int32, (step_rows, LANES), 1)

    def combine(slots, r, n):
        peak = slots[r, 0, 0:1, :]
        for k in range(1, n):
            peak = jnp.maximum(peak, slots[r, k, 0:1, :])
        total = jnp.zeros_like(peak)
        for k in range(n):
            total = total + slots[r, k, 1:2, :] * jnp.exp(slots[r, k, 0:1, :] - peak)
        return peak + jnp.log(total)

    def row_round(r, col_potential):
        @pl.loop(0, rows // step_rows)
        def _(i):
            at = pl.ds(pl.multiple_of(i * step_rows, step_rows), step_rows)
            x = scores[at, :]
            if col_potential is not None:
                x = x + col_potential
            m = jnp.max(x, axis=1, keepdims=True)
            s = jnp.sum(jnp.exp(x - m), axis=1, keepdims=True)
            tbuf[at, :] = jnp.where(lane == 0, m, s)

        row_slots[r, c, :, :] = tbuf[...].T[0:2, :]
        for k in range(1, nc):
            push(row_slots.at[r, c], row_slots.at[r, c], rs_sem.at[r, k], rr_sem.at[r, c], (d, lax.rem(c + k, nc)))
        for k in range(1, nc):
            src = lax.rem(c + nc - k, nc)
            arrive(row_slots.at[r, src], rs_sem.at[r, k], rr_sem.at[r, src])
        row_potential = -combine(row_slots, r, nc)
        rp_v[...] = jnp.broadcast_to(row_potential, (LANES, rows)).T

    def col_round(r):
        for j in range(cols // LANES):
            at = slice(j * LANES, (j + 1) * LANES)
            x = scores[:, at] + rp_v[...]
            m = jnp.max(x, axis=0, keepdims=True)
            s = jnp.sum(jnp.exp(x - m), axis=0, keepdims=True)
            col_slots[r, d, 0:1, at] = m
            col_slots[r, d, 1:2, at] = s
        for k in range(1, nd):
            push(col_slots.at[r, d], col_slots.at[r, d], cs_sem.at[r, k], cr_sem.at[r, d], (lax.rem(d + k, nd), c))
        for k in range(1, nd):
            src = lax.rem(d + nd - k, nd)
            arrive(col_slots.at[r, src], cs_sem.at[r, k], cr_sem.at[r, src])
        return log_column - combine(col_slots, r, nd)

    col_potential = None
    for r in range(ITERS):
        row_round(r, col_potential)
        col_potential = col_round(r)
    row_round(ITERS, col_potential)

    for j in range(cols // LANES):
        at = slice(j * LANES, (j + 1) * LANES)
        w = jnp.exp(scores[:, at] + rp_v[...] + col_potential[:, at])
        mass_slots[d, :, at] = jnp.sum(w, axis=0, keepdims=True)
        assign_v[:, at] = (w * total_cols).astype(jnp.bfloat16)
    assign_copy = pltpu.make_async_copy(assign_v, assign_out, out_sem.at[0])
    assign_copy.start()
    for k in range(1, nd):
        push(mass_slots.at[d], mass_slots.at[d], ms_sem.at[k], mr_sem.at[d], (lax.rem(d + k, nd), c))

    def partial(q):
        r3 = rows_v[:, :, pl.ds(pl.multiple_of(q * feats, feats), feats)].reshape(rows, feats)
        return lax.dot_general(
            assign_v[...], r3, (((0,), (0,)), ((), ())), preferred_element_type=jnp.float32
        ).astype(jnp.bfloat16)

    for k in reversed(range(1, nd)):
        q = lax.rem(d + k, nd)
        part_send[k, :, :] = partial(q)
        push(part_send.at[k], part_recv.at[d], ps_sem.at[k], pr_sem.at[d], (q, c))
    part_recv[d, :, :] = partial(d)

    for k in range(1, nd):
        src = lax.rem(d + nd - k, nd)
        arrive(mass_slots.at[src], ms_sem.at[k], mr_sem.at[src])
    raw_mass = mass_slots[0]
    for k in range(1, nd):
        raw_mass = raw_mass + mass_slots[k]
    mass_out[...] = raw_mass * total_cols / total_rows
    mass_col = jnp.broadcast_to(raw_mass, (LANES, cols)).T

    for k in range(1, nd):
        src = lax.rem(d + nd - k, nd)
        arrive(part_recv.at[src], ps_sem.at[k], pr_sem.at[src])
    for j in range(feats // LANES):
        at = slice(j * LANES, (j + 1) * LANES)
        sums = part_recv[0, :, at].astype(jnp.float32)
        for k in range(1, nd):
            sums = sums + part_recv[k, :, at].astype(jnp.float32)
        newc_v[:, at] = sums / total_cols / mass_col
    newc_copy = pltpu.make_async_copy(newc_v, newc_out, out_sem.at[1])
    newc_copy.start()
    for copy in sends:
        copy.wait_send()
    assign_copy.wait()
    newc_copy.wait()


def shards(nd, nc, passages, centroids):
    block, width = passages.shape
    cols = centroids.shape[0]
    rows = nc * block
    feats = width // nd
    any_spec = pl.BlockSpec(memory_space=pl.ANY)
    dma = pltpu.SemaphoreType.DMA
    f32, bf16 = jnp.float32, jnp.bfloat16
    assign, masses, newc = pl.pallas_call(
        functools.partial(kernel, nd, nc),
        out_shape=(
            jax.ShapeDtypeStruct((rows, cols), bf16),
            jax.ShapeDtypeStruct((1, cols), f32),
            jax.ShapeDtypeStruct((cols, feats), f32),
        ),
        in_specs=[any_spec, any_spec],
        out_specs=(any_spec, pl.BlockSpec(memory_space=pltpu.VMEM), any_spec),
        scratch_shapes=[
            pltpu.VMEM((nc, block, width), bf16),
            pltpu.VMEM((cols, width), bf16),
            pltpu.VMEM((rows, cols), f32),
            pltpu.VMEM((rows, LANES), f32),
            pltpu.VMEM((rows, LANES), f32),
            pltpu.VMEM((ITERS + 1, nc, 2, rows), f32),
            pltpu.VMEM((ITERS, nd, 2, cols), f32),
            pltpu.VMEM((nd, 1, cols), f32),
            pltpu.VMEM((rows, cols), bf16),
            pltpu.VMEM((nd, cols, feats), bf16),
            pltpu.VMEM((nd, cols, feats), bf16),
            pltpu.VMEM((cols, feats), f32),
            dma((2,)),
            dma((nc,)),
            dma((nc,)),
            dma((ITERS + 1, nc)),
            dma((ITERS + 1, nc)),
            dma((ITERS, nd)),
            dma((ITERS, nd)),
            dma((nd,)),
            dma((nd,)),
            dma((nd,)),
            dma((nd,)),
            dma((2,)),
        ],
        compiler_params=pltpu.CompilerParams(
            collective_id=0, has_side_effects=True, vmem_limit_bytes=52 * 1024 * 1024
        ),
    )(passages, centroids)
    return assign, masses.reshape(cols), newc


def solution(mesh):
    nd, nc = mesh.shape["doc"], mesh.shape["cen"]
    in_specs = (P(("doc", "cen"), None), P("cen", None))
    out_specs = (P("doc", "cen"), P("cen"), P("cen", "doc"))
    return jax.shard_map(
        functools.partial(shards, nd, nc), mesh=mesh, in_specs=in_specs, out_specs=out_specs, check_vma=False
    )
```

```python
import functools
import math

import jax
import jax.numpy as jnp
from jax import lax
from jax.experimental import pallas as pl
from jax.experimental.pallas import tpu as pltpu
from jax.sharding import PartitionSpec as P

ITERS = 3
MESH = pl.DeviceIdType.MESH
LANES = 128


def kernel(
    nd, nc, p_ref, c_ref, assign_out, mass_out, newc_out,
    rows_v, cent_v, scores, rp_v, tbuf, row_slots, col_slots, mass_slots, assign_v, part_send, part_recv, newc_v,
    load_sem, gs_sem, gr_sem, rs_sem, rr_sem, cs_sem, cr_sem, ms_sem, mr_sem, ps_sem, pr_sem, out_sem,
):
    d = lax.axis_index("doc")
    c = lax.axis_index("cen")
    block, width = p_ref.shape
    cols = c_ref.shape[0]
    rows = nc * block
    feats = width // nd
    total_cols = cols * nc
    total_rows = rows * nd
    scale = 1.0 / math.sqrt(width)
    log_column = math.log(total_rows / total_cols)
    sends = []

    load_p = pltpu.make_async_copy(p_ref, rows_v.at[c], load_sem.at[0])
    load_c = pltpu.make_async_copy(c_ref, cent_v, load_sem.at[1])
    load_p.start()
    load_c.start()

    barrier = pltpu.get_barrier_semaphore()
    for k in range(1, nc):
        pl.semaphore_signal(barrier, inc=1, device_id=(d, lax.rem(c + k, nc)), device_id_type=MESH)
    for k in range(1, nd):
        pl.semaphore_signal(barrier, inc=1, device_id=(lax.rem(d + k, nd), c), device_id_type=MESH)
    pl.semaphore_wait(barrier, nc + nd - 2)
    load_p.wait()

    def push(src, dst, send, recv, where):
        copy = pltpu.make_async_remote_copy(
            src_ref=src, dst_ref=dst, send_sem=send, recv_sem=recv, device_id=where, device_id_type=MESH
        )
        copy.start()
        sends.append(copy)

    def arrive(ref, send, recv):
        pltpu.make_async_remote_copy(
            src_ref=ref, dst_ref=ref, send_sem=send, recv_sem=recv, device_id=(d, c), device_id_type=MESH
        ).wait_recv()

    mate = c + 1 - 2 * lax.rem(c, 2)
    half = nc // 2
    for k in range(1, half):
        push(rows_v.at[c], rows_v.at[c], gs_sem.at[k], gr_sem.at[c], (d, lax.rem(c + 2 * k, nc)))
    push(rows_v.at[c], rows_v.at[c], gs_sem.at[0], gr_sem.at[c], (d, mate))
    order = [k for pair in zip(range(1, half), reversed(range(1, half))) for k in pair][: half - 1]
    for k in order:
        src = lax.rem(c + nc - 2 * k, nc)
        arrive(rows_v.at[src], gs_sem.at[half + k], gr_sem.at[src])
        push(rows_v.at[src], rows_v.at[src], gs_sem.at[half + k], gr_sem.at[src], (d, mate))
    arrive(rows_v.at[mate], gs_sem.at[0], gr_sem.at[mate])
    for k in range(1, half):
        src = lax.rem(mate + nc - 2 * k, nc)
        arrive(rows_v.at[src], gs_sem.at[0], gr_sem.at[src])
    load_c.wait()

    group_rows = rows_v[...].reshape(rows, width)
    tile = min(256, cols)
    for j in range(cols // tile):
        at = slice(j * tile, (j + 1) * tile)
        scores[:, at] = (
            lax.dot_general(
                group_rows, cent_v[at, :], (((1,), (1,)), ((), ())), preferred_element_type=jnp.float32
            )
            * scale
        )

    step_rows = 64
    lane = lax.broadcasted_iota(jnp.int32, (step_rows, LANES), 1)

    def combine(slots, r, n):
        peak = slots[r, 0, 0:1, :]
        for k in range(1, n):
            peak = jnp.maximum(peak, slots[r, k, 0:1, :])
        total = jnp.zeros_like(peak)
        for k in range(n):
            total = total + slots[r, k, 1:2, :] * jnp.exp(slots[r, k, 0:1, :] - peak)
        return peak + jnp.log(total)

    def row_round(r, col_potential):
        @pl.loop(0, rows // step_rows)
        def _(i):
            at = pl.ds(pl.multiple_of(i * step_rows, step_rows), step_rows)
            x = scores[at, :]
            if col_potential is not None:
                x = x + col_potential
            m = jnp.max(x, axis=1, keepdims=True)
            s = jnp.sum(jnp.exp(x - m), axis=1, keepdims=True)
            tbuf[at, :] = jnp.where(lane == 0, m, s)

        row_slots[r, c, :, :] = tbuf[...].T[0:2, :]
        for k in range(1, nc):
            push(row_slots.at[r, c], row_slots.at[r, c], rs_sem.at[r, k], rr_sem.at[r, c], (d, lax.rem(c + k, nc)))
        for k in range(1, nc):
            src = lax.rem(c + nc - k, nc)
            arrive(row_slots.at[r, src], rs_sem.at[r, k], rr_sem.at[r, src])
        row_potential = -combine(row_slots, r, nc)
        rp_v[...] = jnp.broadcast_to(row_potential, (LANES, rows)).T

    def col_round(r):
        for j in range(cols // LANES):
            at = slice(j * LANES, (j + 1) * LANES)
            x = scores[:, at] + rp_v[...]
            m = jnp.max(x, axis=0, keepdims=True)
            s = jnp.sum(jnp.exp(x - m), axis=0, keepdims=True)
            col_slots[r, d, 0:1, at] = m
            col_slots[r, d, 1:2, at] = s
        for k in range(1, nd):
            push(col_slots.at[r, d], col_slots.at[r, d], cs_sem.at[r, k], cr_sem.at[r, d], (lax.rem(d + k, nd), c))
        for k in range(1, nd):
            src = lax.rem(d + nd - k, nd)
            arrive(col_slots.at[r, src], cs_sem.at[r, k], cr_sem.at[r, src])
        return log_column - combine(col_slots, r, nd)

    col_potential = None
    for r in range(ITERS):
        row_round(r, col_potential)
        col_potential = col_round(r)
    row_round(ITERS, col_potential)

    for j in range(cols // LANES):
        at = slice(j * LANES, (j + 1) * LANES)
        w = jnp.exp(scores[:, at] + rp_v[...] + col_potential[:, at])
        mass_slots[d, :, at] = jnp.sum(w, axis=0, keepdims=True)
        assign_v[:, at] = (w * total_cols).astype(jnp.bfloat16)
    assign_copy = pltpu.make_async_copy(assign_v, assign_out, out_sem.at[0])
    assign_copy.start()
    for k in range(1, nd):
        push(mass_slots.at[d], mass_slots.at[d], ms_sem.at[k], mr_sem.at[d], (lax.rem(d + k, nd), c))

    def partial(q):
        r3 = rows_v[:, :, pl.ds(pl.multiple_of(q * feats, feats), feats)].reshape(rows, feats)
        return lax.dot_general(
            assign_v[...], r3, (((0,), (0,)), ((), ())), preferred_element_type=jnp.float32
        ).astype(jnp.bfloat16)

    for k in reversed(range(1, nd)):
        q = lax.rem(d + k, nd)
        part_send[k, :, :] = partial(q)
        push(part_send.at[k], part_recv.at[d], ps_sem.at[k], pr_sem.at[d], (q, c))
    part_recv[d, :, :] = partial(d)

    for k in range(1, nd):
        src = lax.rem(d + nd - k, nd)
        arrive(mass_slots.at[src], ms_sem.at[k], mr_sem.at[src])
    raw_mass = mass_slots[0]
    for k in range(1, nd):
        raw_mass = raw_mass + mass_slots[k]
    mass_out[...] = raw_mass * total_cols / total_rows
    mass_col = jnp.broadcast_to(raw_mass, (LANES, cols)).T

    for k in range(1, nd):
        src = lax.rem(d + nd - k, nd)
        arrive(part_recv.at[src], ps_sem.at[k], pr_sem.at[src])
    for j in range(feats // LANES):
        at = slice(j * LANES, (j + 1) * LANES)
        sums = part_recv[0, :, at].astype(jnp.float32)
        for k in range(1, nd):
            sums = sums + part_recv[k, :, at].astype(jnp.float32)
        newc_v[:, at] = sums / total_cols / mass_col
    newc_copy = pltpu.make_async_copy(newc_v, newc_out, out_sem.at[1])
    newc_copy.start()
    for copy in sends:
        copy.wait_send()
    assign_copy.wait()
    newc_copy.wait()


def wide_kernel(
    nd, nc, p_ref, c_ref, assign_out, mass_out, newc_out,
    rows_v, cent_v, scores, rp_v, tbuf, row_slots, col_slots, rp_slots, mass_slots, assign_v, newc_v,
    load_sem, gs_sem, gr_sem, ds_sem, dr_sem, rs_sem, rr_sem, cs_sem, cr_sem, ps_sem, pr_sem, out_sem,
):
    d = lax.axis_index("doc")
    c = lax.axis_index("cen")
    block, width = p_ref.shape
    cols = c_ref.shape[0]
    rows = nc * block
    feats = width // nd
    total_cols = cols * nc
    total_rows = rows * nd
    scale = 1.0 / math.sqrt(width)
    log_column = math.log(total_rows / total_cols)
    sends = []

    load_p = pltpu.make_async_copy(p_ref, rows_v.at[d, c], load_sem.at[0])
    load_c = pltpu.make_async_copy(c_ref, cent_v, load_sem.at[1])
    load_p.start()
    load_c.start()

    barrier = pltpu.get_barrier_semaphore()
    for k in range(1, nc):
        pl.semaphore_signal(barrier, inc=1, device_id=(d, lax.rem(c + k, nc)), device_id_type=MESH)
    for k in range(1, nd):
        pl.semaphore_signal(barrier, inc=1, device_id=(lax.rem(d + k, nd), c), device_id_type=MESH)
    pl.semaphore_wait(barrier, nc + nd - 2)
    load_p.wait()

    def push(src, dst, send, recv, where):
        copy = pltpu.make_async_remote_copy(
            src_ref=src, dst_ref=dst, send_sem=send, recv_sem=recv, device_id=where, device_id_type=MESH
        )
        copy.start()
        sends.append(copy)

    def arrive(ref, send, recv):
        pltpu.make_async_remote_copy(
            src_ref=ref, dst_ref=ref, send_sem=send, recv_sem=recv, device_id=(d, c), device_id_type=MESH
        ).wait_recv()

    mate = c + 1 - 2 * lax.rem(c, 2)
    half = nc // 2

    def to_docs(b, slot):
        for k in range(1, nd):
            push(rows_v.at[d, b], rows_v.at[d, b], ds_sem.at[k, slot], dr_sem.at[d, b], (lax.rem(d + k, nd), c))

    own = rows_v.at[d, c]
    for k in range(1, half):
        push(own, own, gs_sem.at[k], gr_sem.at[c], (d, lax.rem(c + 2 * k, nc)))
    push(own, own, gs_sem.at[0], gr_sem.at[c], (d, mate))
    to_docs(c, 0)
    order = [k for pair in zip(range(1, half), reversed(range(1, half))) for k in pair][: half - 1]
    for k in order:
        src = lax.rem(c + nc - 2 * k, nc)
        got = rows_v.at[d, src]
        arrive(got, gs_sem.at[half + k], gr_sem.at[src])
        push(got, got, gs_sem.at[half + k], gr_sem.at[src], (d, mate))
        to_docs(src, k)
    arrive(rows_v.at[d, mate], gs_sem.at[0], gr_sem.at[mate])
    for k in range(1, half):
        src = lax.rem(mate + nc - 2 * k, nc)
        arrive(rows_v.at[d, src], gs_sem.at[0], gr_sem.at[src])
    load_c.wait()

    def relay():
        for k in range(half):
            b = lax.rem(c + nc - 2 * k, nc)
            for q in range(1, nd):
                src = lax.rem(d + nd - q, nd)
                got = rows_v.at[src, b]
                arrive(got, ds_sem.at[0, k], dr_sem.at[src, b])
                push(got, got, ds_sem.at[nd + q, k], dr_sem.at[src, b], (d, mate))

    def arrive_doc(dd):
        for k in range(half):
            b = lax.rem(mate + nc - 2 * k, nc)
            arrive(rows_v.at[dd, b], ds_sem.at[0, k], dr_sem.at[dd, b])

    tile = min(256, cols)

    def score(dd):
        for j in range(cols // tile):
            at = slice(j * tile, (j + 1) * tile)
            scores[dd, :, at] = (
                lax.dot_general(
                    rows_v[dd].reshape(rows, width),
                    cent_v[at, :],
                    (((1,), (1,)), ((), ())),
                    preferred_element_type=jnp.float32,
                )
                * scale
            )

    score(d)

    step_rows = 64
    lane = lax.broadcasted_iota(jnp.int32, (step_rows, LANES), 1)

    def combine(slots, r, n):
        peak = slots[r, 0, 0:1, :]
        for k in range(1, n):
            peak = jnp.maximum(peak, slots[r, k, 0:1, :])
        total = jnp.zeros_like(peak)
        for k in range(n):
            total = total + slots[r, k, 1:2, :] * jnp.exp(slots[r, k, 0:1, :] - peak)
        return peak + jnp.log(total)

    def row_round(r, col_potential, meanwhile):
        @pl.loop(0, rows // step_rows)
        def _(i):
            at = pl.ds(pl.multiple_of(i * step_rows, step_rows), step_rows)
            x = scores[d, at, :]
            if col_potential is not None:
                x = x + col_potential
            m = jnp.max(x, axis=1, keepdims=True)
            s = jnp.sum(jnp.exp(x - m), axis=1, keepdims=True)
            tbuf[at, :] = jnp.where(lane == 0, m, s)

        row_slots[r, c, :, :] = tbuf[...].T[0:2, :]
        for k in range(1, nc):
            push(row_slots.at[r, c], row_slots.at[r, c], rs_sem.at[r, k], rr_sem.at[r, c], (d, lax.rem(c + k, nc)))
        meanwhile()
        for k in range(1, nc):
            src = lax.rem(c + nc - k, nc)
            arrive(row_slots.at[r, src], rs_sem.at[r, k], rr_sem.at[r, src])
        row_potential = -combine(row_slots, r, nc)
        rp_v[...] = jnp.broadcast_to(row_potential, (LANES, rows)).T
        return row_potential

    def col_round(r, meanwhile):
        for j in range(cols // LANES):
            at = slice(j * LANES, (j + 1) * LANES)
            x = scores[d, :, at] + rp_v[...]
            m = jnp.max(x, axis=0, keepdims=True)
            s = jnp.sum(jnp.exp(x - m), axis=0, keepdims=True)
            col_slots[r, d, 0:1, at] = m
            col_slots[r, d, 1:2, at] = s
        for k in range(1, nd):
            push(col_slots.at[r, d], col_slots.at[r, d], cs_sem.at[r, k], cr_sem.at[r, d], (lax.rem(d + k, nd), c))
        meanwhile()
        for k in range(1, nd):
            src = lax.rem(d + nd - k, nd)
            arrive(col_slots.at[r, src], cs_sem.at[r, k], cr_sem.at[r, src])
        return log_column - combine(col_slots, r, nd)

    def score_other(q):
        dd = lax.rem(d + q, nd)
        arrive_doc(dd)
        score(dd)

    work = [lambda: None, lambda: None, relay] + [functools.partial(score_other, q) for q in range(1, nd)]
    work += [lambda: None] * (2 * ITERS + 1 - len(work))
    col_potential = None
    for r in range(ITERS):
        row_round(r, col_potential, work[2 * r])
        col_potential = col_round(r, work[2 * r + 1])

    def finish():
        for extra in work[2 * ITERS :]:
            extra()

    rp_slots[d] = row_round(ITERS, col_potential, finish)
    for k in range(1, nd):
        push(rp_slots.at[d], rp_slots.at[d], ps_sem.at[k], pr_sem.at[d], (lax.rem(d + k, nd), c))

    assign_copy = pltpu.make_async_copy(assign_v.at[d], assign_out, out_sem.at[0])
    my_feats = pl.ds(pl.multiple_of(d * feats, feats), feats)
    for k in range(nd):
        dd = lax.rem(d + k, nd)
        if k:
            arrive(rp_slots.at[dd], ps_sem.at[0], pr_sem.at[dd])
            rp_v[...] = jnp.broadcast_to(rp_slots[dd], (LANES, rows)).T
        for j in range(cols // LANES):
            at = slice(j * LANES, (j + 1) * LANES)
            w = jnp.exp(scores[dd, :, at] + rp_v[...] + col_potential[:, at])
            mass_slots[dd, :, at] = jnp.sum(w, axis=0, keepdims=True)
            assign_v[dd, :, at] = (w * total_cols).astype(jnp.bfloat16)
        if not k:
            assign_copy.start()
        part = lax.dot_general(
            assign_v[dd],
            rows_v[dd, :, :, my_feats].reshape(rows, feats),
            (((0,), (0,)), ((), ())),
            preferred_element_type=jnp.float32,
        ).astype(jnp.bfloat16).astype(jnp.float32)
        newc_v[...] = newc_v[...] + part if k else part

    raw_mass = mass_slots[0]
    for k in range(1, nd):
        raw_mass = raw_mass + mass_slots[k]
    mass_out[...] = raw_mass * total_cols / total_rows
    mass_col = jnp.broadcast_to(raw_mass, (LANES, cols)).T
    for j in range(feats // LANES):
        at = slice(j * LANES, (j + 1) * LANES)
        newc_v[:, at] = newc_v[:, at] / total_cols / mass_col
    newc_copy = pltpu.make_async_copy(newc_v, newc_out, out_sem.at[1])
    newc_copy.start()
    for copy in sends:
        copy.wait_send()
    assign_copy.wait()
    newc_copy.wait()


def shards(nd, nc, passages, centroids):
    block, width = passages.shape
    cols = centroids.shape[0]
    rows = nc * block
    feats = width // nd
    any_spec = pl.BlockSpec(memory_space=pl.ANY)
    dma = pltpu.SemaphoreType.DMA
    f32, bf16 = jnp.float32, jnp.bfloat16
    wide = nd * rows * cols <= 2**22 and nc % 2 == 0
    if wide:
        body = wide_kernel
        scratch = [
            pltpu.VMEM((nd, nc, block, width), bf16),
            pltpu.VMEM((cols, width), bf16),
            pltpu.VMEM((nd, rows, cols), f32),
            pltpu.VMEM((rows, LANES), f32),
            pltpu.VMEM((rows, LANES), f32),
            pltpu.VMEM((ITERS + 1, nc, 2, rows), f32),
            pltpu.VMEM((ITERS, nd, 2, cols), f32),
            pltpu.VMEM((nd, 1, rows), f32),
            pltpu.VMEM((nd, 1, cols), f32),
            pltpu.VMEM((nd, rows, cols), bf16),
            pltpu.VMEM((cols, feats), f32),
            dma((2,)),
            dma((nc,)),
            dma((nc,)),
            dma((2 * nd, nc // 2)),
            dma((nd, nc)),
            dma((ITERS + 1, nc)),
            dma((ITERS + 1, nc)),
            dma((ITERS, nd)),
            dma((ITERS, nd)),
            dma((nd,)),
            dma((nd,)),
            dma((2,)),
        ]
    else:
        body = kernel
        scratch = [
            pltpu.VMEM((nc, block, width), bf16),
            pltpu.VMEM((cols, width), bf16),
            pltpu.VMEM((rows, cols), f32),
            pltpu.VMEM((rows, LANES), f32),
            pltpu.VMEM((rows, LANES), f32),
            pltpu.VMEM((ITERS + 1, nc, 2, rows), f32),
            pltpu.VMEM((ITERS, nd, 2, cols), f32),
            pltpu.VMEM((nd, 1, cols), f32),
            pltpu.VMEM((rows, cols), bf16),
            pltpu.VMEM((nd, cols, feats), bf16),
            pltpu.VMEM((nd, cols, feats), bf16),
            pltpu.VMEM((cols, feats), f32),
            dma((2,)),
            dma((nc,)),
            dma((nc,)),
            dma((ITERS + 1, nc)),
            dma((ITERS + 1, nc)),
            dma((ITERS, nd)),
            dma((ITERS, nd)),
            dma((nd,)),
            dma((nd,)),
            dma((nd,)),
            dma((nd,)),
            dma((2,)),
        ]
    assign, masses, newc = pl.pallas_call(
        functools.partial(body, nd, nc),
        out_shape=(
            jax.ShapeDtypeStruct((rows, cols), bf16),
            jax.ShapeDtypeStruct((1, cols), f32),
            jax.ShapeDtypeStruct((cols, feats), f32),
        ),
        in_specs=[pl.BlockSpec(memory_space=pltpu.MemorySpace.HBM)] * 2,
        out_specs=(any_spec, pl.BlockSpec(memory_space=pltpu.VMEM), any_spec),
        scratch_shapes=scratch,
        compiler_params=pltpu.CompilerParams(
            collective_id=0, has_side_effects=True, vmem_limit_bytes=52 * 1024 * 1024
        ),
    )(passages, centroids)
    return assign, masses.reshape(cols), newc


def solution(mesh):
    nd, nc = mesh.shape["doc"], mesh.shape["cen"]
    in_specs = (P(("doc", "cen"), None), P("cen", None))
    out_specs = (P("doc", "cen"), P("cen"), P("cen", "doc"))
    return jax.shard_map(
        functools.partial(shards, nd, nc), mesh=mesh, in_specs=in_specs, out_specs=out_specs, check_vma=False
    )
```

```python
import functools
import math

import jax
import jax.numpy as jnp
from jax import lax
from jax.experimental import pallas as pl
from jax.experimental.pallas import tpu as pltpu
from jax.sharding import PartitionSpec as P

ITERS = 3
MESH = pl.DeviceIdType.MESH
LANES = 128


def kernel(
    nd, nc, p_ref, c_ref, assign_out, mass_out, newc_out,
    rows_v, cent_v, scores, rp_v, tbuf, row_slots, col_slots, mass_slots, assign_v, part_send, part_recv, newc_v,
    load_sem, gs_sem, gr_sem, rs_sem, rr_sem, cs_sem, cr_sem, ms_sem, mr_sem, ps_sem, pr_sem, out_sem,
):
    d = lax.axis_index("doc")
    c = lax.axis_index("cen")
    block, width = p_ref.shape
    cols = c_ref.shape[0]
    rows = nc * block
    feats = width // nd
    total_cols = cols * nc
    total_rows = rows * nd
    scale = 1.0 / math.sqrt(width)
    log_column = math.log(total_rows / total_cols)
    sends = []

    load_p = pltpu.make_async_copy(p_ref, rows_v.at[c], load_sem.at[0])
    load_c = pltpu.make_async_copy(c_ref, cent_v, load_sem.at[1])
    load_p.start()
    load_c.start()

    barrier = pltpu.get_barrier_semaphore()
    for k in range(1, nc):
        pl.semaphore_signal(barrier, inc=1, device_id=(d, lax.rem(c + k, nc)), device_id_type=MESH)
    for k in range(1, nd):
        pl.semaphore_signal(barrier, inc=1, device_id=(lax.rem(d + k, nd), c), device_id_type=MESH)
    pl.semaphore_wait(barrier, nc + nd - 2)
    load_p.wait()

    def push(src, dst, send, recv, where):
        copy = pltpu.make_async_remote_copy(
            src_ref=src, dst_ref=dst, send_sem=send, recv_sem=recv, device_id=where, device_id_type=MESH
        )
        copy.start()
        sends.append(copy)

    def arrive(ref, send, recv):
        pltpu.make_async_remote_copy(
            src_ref=ref, dst_ref=ref, send_sem=send, recv_sem=recv, device_id=(d, c), device_id_type=MESH
        ).wait_recv()

    mate = c + 1 - 2 * lax.rem(c, 2)
    half = nc // 2
    for k in range(1, half):
        push(rows_v.at[c], rows_v.at[c], gs_sem.at[k], gr_sem.at[c], (d, lax.rem(c + 2 * k, nc)))
    push(rows_v.at[c], rows_v.at[c], gs_sem.at[0], gr_sem.at[c], (d, mate))
    order = [k for pair in zip(range(1, half), reversed(range(1, half))) for k in pair][: half - 1]
    for k in order:
        src = lax.rem(c + nc - 2 * k, nc)
        arrive(rows_v.at[src], gs_sem.at[half + k], gr_sem.at[src])
        push(rows_v.at[src], rows_v.at[src], gs_sem.at[half + k], gr_sem.at[src], (d, mate))
    arrive(rows_v.at[mate], gs_sem.at[0], gr_sem.at[mate])
    for k in range(1, half):
        src = lax.rem(mate + nc - 2 * k, nc)
        arrive(rows_v.at[src], gs_sem.at[0], gr_sem.at[src])
    load_c.wait()

    group_rows = rows_v[...].reshape(rows, width)
    tile = min(256, cols)
    for j in range(cols // tile):
        at = slice(j * tile, (j + 1) * tile)
        scores[:, at] = (
            lax.dot_general(
                group_rows, cent_v[at, :], (((1,), (1,)), ((), ())), preferred_element_type=jnp.float32
            )
            * scale
        )

    step_rows = 64
    lane = lax.broadcasted_iota(jnp.int32, (step_rows, LANES), 1)

    def combine(slots, r, n):
        peak = slots[r, 0, 0:1, :]
        for k in range(1, n):
            peak = jnp.maximum(peak, slots[r, k, 0:1, :])
        total = jnp.zeros_like(peak)
        for k in range(n):
            total = total + slots[r, k, 1:2, :] * jnp.exp(slots[r, k, 0:1, :] - peak)
        return peak + jnp.log(total)

    def row_round(r, col_potential):
        @pl.loop(0, rows // step_rows)
        def _(i):
            at = pl.ds(pl.multiple_of(i * step_rows, step_rows), step_rows)
            x = scores[at, :]
            if col_potential is not None:
                x = x + col_potential
            m = jnp.max(x, axis=1, keepdims=True)
            s = jnp.sum(jnp.exp(x - m), axis=1, keepdims=True)
            tbuf[at, :] = jnp.where(lane == 0, m, s)

        row_slots[r, c, :, :] = tbuf[...].T[0:2, :]
        for k in range(1, nc):
            push(row_slots.at[r, c], row_slots.at[r, c], rs_sem.at[r, k], rr_sem.at[r, c], (d, lax.rem(c + k, nc)))
        for k in range(1, nc):
            src = lax.rem(c + nc - k, nc)
            arrive(row_slots.at[r, src], rs_sem.at[r, k], rr_sem.at[r, src])
        row_potential = -combine(row_slots, r, nc)
        rp_v[...] = jnp.broadcast_to(row_potential, (LANES, rows)).T

    def col_round(r):
        for j in range(cols // LANES):
            at = slice(j * LANES, (j + 1) * LANES)
            x = scores[:, at] + rp_v[...]
            m = jnp.max(x, axis=0, keepdims=True)
            s = jnp.sum(jnp.exp(x - m), axis=0, keepdims=True)
            col_slots[r, d, 0:1, at] = m
            col_slots[r, d, 1:2, at] = s
        for k in range(1, nd):
            push(col_slots.at[r, d], col_slots.at[r, d], cs_sem.at[r, k], cr_sem.at[r, d], (lax.rem(d + k, nd), c))
        for k in range(1, nd):
            src = lax.rem(d + nd - k, nd)
            arrive(col_slots.at[r, src], cs_sem.at[r, k], cr_sem.at[r, src])
        return log_column - combine(col_slots, r, nd)

    col_potential = None
    for r in range(ITERS):
        row_round(r, col_potential)
        col_potential = col_round(r)
    row_round(ITERS, col_potential)

    for j in range(cols // LANES):
        at = slice(j * LANES, (j + 1) * LANES)
        w = jnp.exp(scores[:, at] + rp_v[...] + col_potential[:, at])
        mass_slots[d, :, at] = jnp.sum(w, axis=0, keepdims=True)
        assign_v[:, at] = (w * total_cols).astype(jnp.bfloat16)
    assign_copy = pltpu.make_async_copy(assign_v, assign_out, out_sem.at[0])
    assign_copy.start()
    for k in range(1, nd):
        push(mass_slots.at[d], mass_slots.at[d], ms_sem.at[k], mr_sem.at[d], (lax.rem(d + k, nd), c))

    def partial(q):
        r3 = rows_v[:, :, pl.ds(pl.multiple_of(q * feats, feats), feats)].reshape(rows, feats)
        return lax.dot_general(
            assign_v[...], r3, (((0,), (0,)), ((), ())), preferred_element_type=jnp.float32
        ).astype(jnp.bfloat16)

    for k in reversed(range(1, nd)):
        q = lax.rem(d + k, nd)
        part_send[k, :, :] = partial(q)
        push(part_send.at[k], part_recv.at[d], ps_sem.at[k], pr_sem.at[d], (q, c))
    part_recv[d, :, :] = partial(d)

    for k in range(1, nd):
        src = lax.rem(d + nd - k, nd)
        arrive(mass_slots.at[src], ms_sem.at[k], mr_sem.at[src])
    raw_mass = mass_slots[0]
    for k in range(1, nd):
        raw_mass = raw_mass + mass_slots[k]
    mass_out[...] = raw_mass * total_cols / total_rows
    mass_col = jnp.broadcast_to(raw_mass, (LANES, cols)).T

    for k in range(1, nd):
        src = lax.rem(d + nd - k, nd)
        arrive(part_recv.at[src], ps_sem.at[k], pr_sem.at[src])
    for j in range(feats // LANES):
        at = slice(j * LANES, (j + 1) * LANES)
        sums = part_recv[0, :, at].astype(jnp.float32)
        for k in range(1, nd):
            sums = sums + part_recv[k, :, at].astype(jnp.float32)
        newc_v[:, at] = sums / total_cols / mass_col
    newc_copy = pltpu.make_async_copy(newc_v, newc_out, out_sem.at[1])
    newc_copy.start()
    for copy in sends:
        copy.wait_send()
    assign_copy.wait()
    newc_copy.wait()


def wide_kernel(
    nd, nc, p_ref, c_ref, assign_out, mass_out, newc_out,
    rows_v, cent_v, scores, rp_v, tbuf, row_slots, col_slots, peak_v, mass_slots, assign_v, newc_v,
    load_sem, gs_sem, gr_sem, ds_sem, dr_sem, rs_sem, rr_sem, cs_sem, cr_sem, out_sem,
):
    d = lax.axis_index("doc")
    c = lax.axis_index("cen")
    block, width = p_ref.shape
    cols = c_ref.shape[0]
    rows = nc * block
    feats = width // nd
    total_cols = cols * nc
    total_rows = rows * nd
    scale = 1.0 / math.sqrt(width)
    log_column = math.log(total_rows / total_cols)
    sends = []

    load_p = pltpu.make_async_copy(p_ref, rows_v.at[d, c], load_sem.at[0])
    load_c = pltpu.make_async_copy(c_ref, cent_v, load_sem.at[1])
    load_p.start()
    load_c.start()

    barrier = pltpu.get_barrier_semaphore()
    for k in range(1, nc):
        pl.semaphore_signal(barrier, inc=1, device_id=(d, lax.rem(c + k, nc)), device_id_type=MESH)
    for k in range(1, nd):
        pl.semaphore_signal(barrier, inc=1, device_id=(lax.rem(d + k, nd), c), device_id_type=MESH)
    pl.semaphore_wait(barrier, nc + nd - 2)
    load_p.wait()

    def push(src, dst, send, recv, where):
        copy = pltpu.make_async_remote_copy(
            src_ref=src, dst_ref=dst, send_sem=send, recv_sem=recv, device_id=where, device_id_type=MESH
        )
        copy.start()
        sends.append(copy)

    def arrive(ref, send, recv):
        pltpu.make_async_remote_copy(
            src_ref=ref, dst_ref=ref, send_sem=send, recv_sem=recv, device_id=(d, c), device_id_type=MESH
        ).wait_recv()

    mate = c + 1 - 2 * lax.rem(c, 2)
    half = nc // 2

    def to_docs(b, slot):
        for k in range(1, nd):
            push(rows_v.at[d, b], rows_v.at[d, b], ds_sem.at[k, slot], dr_sem.at[d, b], (lax.rem(d + k, nd), c))

    own = rows_v.at[d, c]
    for k in range(1, half):
        push(own, own, gs_sem.at[k], gr_sem.at[c], (d, lax.rem(c + 2 * k, nc)))
    push(own, own, gs_sem.at[0], gr_sem.at[c], (d, mate))
    to_docs(c, 0)
    order = [k for pair in zip(range(1, half), reversed(range(1, half))) for k in pair][: half - 1]
    for k in order:
        src = lax.rem(c + nc - 2 * k, nc)
        got = rows_v.at[d, src]
        arrive(got, gs_sem.at[half + k], gr_sem.at[src])
        push(got, got, gs_sem.at[half + k], gr_sem.at[src], (d, mate))
        to_docs(src, k)
    arrive(rows_v.at[d, mate], gs_sem.at[0], gr_sem.at[mate])
    for k in range(1, half):
        src = lax.rem(mate + nc - 2 * k, nc)
        arrive(rows_v.at[d, src], gs_sem.at[0], gr_sem.at[src])
    load_c.wait()

    def relay():
        for k in range(half):
            b = lax.rem(c + nc - 2 * k, nc)
            for q in range(1, nd):
                src = lax.rem(d + nd - q, nd)
                got = rows_v.at[src, b]
                arrive(got, ds_sem.at[0, k], dr_sem.at[src, b])
                push(got, got, ds_sem.at[nd + q, k], dr_sem.at[src, b], (d, mate))

    def arrive_doc(dd):
        for k in range(half):
            b = lax.rem(mate + nc - 2 * k, nc)
            arrive(rows_v.at[dd, b], ds_sem.at[0, k], dr_sem.at[dd, b])

    tile = min(256, cols)

    def score(dd):
        for j in range(cols // tile):
            at = slice(j * tile, (j + 1) * tile)
            scores[dd, :, at] = (
                lax.dot_general(
                    rows_v[dd].reshape(rows, width),
                    cent_v[at, :],
                    (((1,), (1,)), ((), ())),
                    preferred_element_type=jnp.float32,
                )
                * scale
            )

    score(d)

    step_rows = 64
    lane = lax.broadcasted_iota(jnp.int32, (step_rows, LANES), 1)

    def combine(slots, r, n):
        peak = slots[r, 0, 0:1, :]
        for k in range(1, n):
            peak = jnp.maximum(peak, slots[r, k, 0:1, :])
        total = jnp.zeros_like(peak)
        for k in range(n):
            total = total + slots[r, k, 1:2, :] * jnp.exp(slots[r, k, 0:1, :] - peak)
        return peak + jnp.log(total)

    def row_pass(dd, r, col_potential, keep):
        @pl.loop(0, rows // step_rows)
        def _(i):
            at = pl.ds(pl.multiple_of(i * step_rows, step_rows), step_rows)
            x = scores[dd, at, :]
            if col_potential is not None:
                x = x + col_potential
            m = jnp.max(x, axis=1, keepdims=True)
            e = jnp.exp(x - m)
            s = jnp.sum(e, axis=1, keepdims=True)
            tbuf[at, :] = jnp.where(lane == 0, m, s)
            if keep:
                scores[dd, at, :] = e
                peak_v[dd, at, :] = jnp.broadcast_to(m, (step_rows, LANES))

        row_slots[r, c, :, :] = tbuf[...].T[0:2, :]
        for k in range(1, nc):
            push(row_slots.at[r, c], row_slots.at[r, c], rs_sem.at[r, k], rr_sem.at[r, c], (d, lax.rem(c + k, nc)))

    def row_finish(r):
        for k in range(1, nc):
            src = lax.rem(c + nc - k, nc)
            arrive(row_slots.at[r, src], rs_sem.at[r, k], rr_sem.at[r, src])
        row_potential = -combine(row_slots, r, nc)
        return jnp.broadcast_to(row_potential, (LANES, rows)).T

    def col_round(r, meanwhile):
        for j in range(cols // LANES):
            at = slice(j * LANES, (j + 1) * LANES)
            x = scores[d, :, at] + rp_v[...]
            m = jnp.max(x, axis=0, keepdims=True)
            s = jnp.sum(jnp.exp(x - m), axis=0, keepdims=True)
            col_slots[r, d, 0:1, at] = m
            col_slots[r, d, 1:2, at] = s
        for k in range(1, nd):
            push(col_slots.at[r, d], col_slots.at[r, d], cs_sem.at[r, k], cr_sem.at[r, d], (lax.rem(d + k, nd), c))
        meanwhile()
        for k in range(1, nd):
            src = lax.rem(d + nd - k, nd)
            arrive(col_slots.at[r, src], cs_sem.at[r, k], cr_sem.at[r, src])
        return log_column - combine(col_slots, r, nd)

    def score_other(q):
        dd = lax.rem(d + q, nd)
        arrive_doc(dd)
        score(dd)

    work = [lambda: None, lambda: None, relay] + [functools.partial(score_other, q) for q in range(1, nd)]
    work += [lambda: None] * (2 * ITERS - len(work))
    col_potential = None
    for r in range(ITERS):
        row_pass(d, r, col_potential, False)
        work[2 * r]()
        rp_v[...] = row_finish(r)
        col_potential = col_round(r, work[2 * r + 1])
    for extra in work[2 * ITERS :]:
        extra()

    for q in range(nd):
        row_pass(lax.rem(d + q, nd), ITERS + q, col_potential, True)
    assign_copy = pltpu.make_async_copy(assign_v.at[d], assign_out, out_sem.at[0])
    my_feats = pl.ds(pl.multiple_of(d * feats, feats), feats)
    for q in range(nd):
        dd = lax.rem(d + q, nd)
        rp_v[...] = jnp.exp(peak_v[dd] + row_finish(ITERS + q))
        for j in range(cols // LANES):
            at = slice(j * LANES, (j + 1) * LANES)
            w = scores[dd, :, at] * rp_v[...]
            mass_slots[dd, :, at] = jnp.sum(w, axis=0, keepdims=True)
            assign_v[dd, :, at] = (w * total_cols).astype(jnp.bfloat16)
        if not q:
            assign_copy.start()
        part = lax.dot_general(
            assign_v[dd],
            rows_v[dd, :, :, my_feats].reshape(rows, feats),
            (((0,), (0,)), ((), ())),
            preferred_element_type=jnp.float32,
        ).astype(jnp.bfloat16).astype(jnp.float32)
        newc_v[...] = newc_v[...] + part if q else part

    raw_mass = mass_slots[0]
    for k in range(1, nd):
        raw_mass = raw_mass + mass_slots[k]
    mass_out[...] = raw_mass * total_cols / total_rows
    mass_col = jnp.broadcast_to(raw_mass, (LANES, cols)).T
    for j in range(feats // LANES):
        at = slice(j * LANES, (j + 1) * LANES)
        newc_v[:, at] = newc_v[:, at] / total_cols / mass_col
    newc_copy = pltpu.make_async_copy(newc_v, newc_out, out_sem.at[1])
    newc_copy.start()
    for copy in sends:
        copy.wait_send()
    assign_copy.wait()
    newc_copy.wait()


def shards(nd, nc, passages, centroids):
    block, width = passages.shape
    cols = centroids.shape[0]
    rows = nc * block
    feats = width // nd
    any_spec = pl.BlockSpec(memory_space=pl.ANY)
    dma = pltpu.SemaphoreType.DMA
    f32, bf16 = jnp.float32, jnp.bfloat16
    wide = nd * rows * cols <= 2**22 and nc % 2 == 0
    if wide:
        body = wide_kernel
        limit = 28 * 1024 * 1024
        scratch = [
            pltpu.VMEM((nd, nc, block, width), bf16),
            pltpu.VMEM((cols, width), bf16),
            pltpu.VMEM((nd, rows, cols), f32),
            pltpu.VMEM((rows, LANES), f32),
            pltpu.VMEM((rows, LANES), f32),
            pltpu.VMEM((ITERS + nd, nc, 2, rows), f32),
            pltpu.VMEM((ITERS, nd, 2, cols), f32),
            pltpu.VMEM((nd, rows, LANES), f32),
            pltpu.VMEM((nd, 1, cols), f32),
            pltpu.VMEM((nd, rows, cols), bf16),
            pltpu.VMEM((cols, feats), f32),
            dma((2,)),
            dma((nc,)),
            dma((nc,)),
            dma((2 * nd, nc // 2)),
            dma((nd, nc)),
            dma((ITERS + nd, nc)),
            dma((ITERS + nd, nc)),
            dma((ITERS, nd)),
            dma((ITERS, nd)),
            dma((2,)),
        ]
    else:
        body = kernel
        limit = 52 * 1024 * 1024
        scratch = [
            pltpu.VMEM((nc, block, width), bf16),
            pltpu.VMEM((cols, width), bf16),
            pltpu.VMEM((rows, cols), f32),
            pltpu.VMEM((rows, LANES), f32),
            pltpu.VMEM((rows, LANES), f32),
            pltpu.VMEM((ITERS + 1, nc, 2, rows), f32),
            pltpu.VMEM((ITERS, nd, 2, cols), f32),
            pltpu.VMEM((nd, 1, cols), f32),
            pltpu.VMEM((rows, cols), bf16),
            pltpu.VMEM((nd, cols, feats), bf16),
            pltpu.VMEM((nd, cols, feats), bf16),
            pltpu.VMEM((cols, feats), f32),
            dma((2,)),
            dma((nc,)),
            dma((nc,)),
            dma((ITERS + 1, nc)),
            dma((ITERS + 1, nc)),
            dma((ITERS, nd)),
            dma((ITERS, nd)),
            dma((nd,)),
            dma((nd,)),
            dma((nd,)),
            dma((nd,)),
            dma((2,)),
        ]
    assign, masses, newc = pl.pallas_call(
        functools.partial(body, nd, nc),
        out_shape=(
            jax.ShapeDtypeStruct((rows, cols), bf16),
            jax.ShapeDtypeStruct((1, cols), f32),
            jax.ShapeDtypeStruct((cols, feats), f32),
        ),
        in_specs=[pl.BlockSpec(memory_space=pltpu.MemorySpace.HBM)] * 2,
        out_specs=(any_spec, pl.BlockSpec(memory_space=pltpu.VMEM), any_spec),
        scratch_shapes=scratch,
        compiler_params=pltpu.CompilerParams(
            collective_id=0, has_side_effects=True, vmem_limit_bytes=limit
        ),
    )(passages, centroids)
    return assign, masses.reshape(cols), newc


def solution(mesh):
    nd, nc = mesh.shape["doc"], mesh.shape["cen"]
    in_specs = (P(("doc", "cen"), None), P("cen", None))
    out_specs = (P("doc", "cen"), P("cen"), P("cen", "doc"))
    return jax.shard_map(
        functools.partial(shards, nd, nc), mesh=mesh, in_specs=in_specs, out_specs=out_specs, check_vma=False
    )
```

```python
import functools
import math

import jax
import jax.numpy as jnp
from jax import lax
from jax.experimental import pallas as pl
from jax.experimental.pallas import tpu as pltpu
from jax.sharding import PartitionSpec as P

ITERS = 3
MESH = pl.DeviceIdType.MESH
LANES = 128


def kernel(
    nd, nc, p_ref, c_ref, assign_out, mass_out, newc_out,
    rows_v, cent_v, scores, rp_v, tbuf, row_slots, col_slots, mass_slots, assign_v, part_send, part_recv, newc_v,
    load_sem, gs_sem, gr_sem, rs_sem, rr_sem, cs_sem, cr_sem, ms_sem, mr_sem, ps_sem, pr_sem, out_sem,
):
    d = lax.axis_index("doc")
    c = lax.axis_index("cen")
    block, width = p_ref.shape
    cols = c_ref.shape[0]
    rows = nc * block
    feats = width // nd
    total_cols = cols * nc
    total_rows = rows * nd
    scale = 1.0 / math.sqrt(width)
    log_column = math.log(total_rows / total_cols)
    sends = []

    load_p = pltpu.make_async_copy(p_ref, rows_v.at[c], load_sem.at[0])
    load_c = pltpu.make_async_copy(c_ref, cent_v, load_sem.at[1])
    load_p.start()
    load_c.start()

    barrier = pltpu.get_barrier_semaphore()
    for k in range(1, nc):
        pl.semaphore_signal(barrier, inc=1, device_id=(d, lax.rem(c + k, nc)), device_id_type=MESH)
    for k in range(1, nd):
        pl.semaphore_signal(barrier, inc=1, device_id=(lax.rem(d + k, nd), c), device_id_type=MESH)
    pl.semaphore_wait(barrier, nc + nd - 2)
    load_p.wait()

    def push(src, dst, send, recv, where):
        copy = pltpu.make_async_remote_copy(
            src_ref=src, dst_ref=dst, send_sem=send, recv_sem=recv, device_id=where, device_id_type=MESH
        )
        copy.start()
        sends.append(copy)

    def arrive(ref, send, recv):
        pltpu.make_async_remote_copy(
            src_ref=ref, dst_ref=ref, send_sem=send, recv_sem=recv, device_id=(d, c), device_id_type=MESH
        ).wait_recv()

    mate = c + 1 - 2 * lax.rem(c, 2)
    half = nc // 2
    for k in range(1, half):
        push(rows_v.at[c], rows_v.at[c], gs_sem.at[k], gr_sem.at[c], (d, lax.rem(c + 2 * k, nc)))
    push(rows_v.at[c], rows_v.at[c], gs_sem.at[0], gr_sem.at[c], (d, mate))
    order = [k for pair in zip(range(1, half), reversed(range(1, half))) for k in pair][: half - 1]
    for k in order:
        src = lax.rem(c + nc - 2 * k, nc)
        arrive(rows_v.at[src], gs_sem.at[half + k], gr_sem.at[src])
        push(rows_v.at[src], rows_v.at[src], gs_sem.at[half + k], gr_sem.at[src], (d, mate))
    arrive(rows_v.at[mate], gs_sem.at[0], gr_sem.at[mate])
    for k in range(1, half):
        src = lax.rem(mate + nc - 2 * k, nc)
        arrive(rows_v.at[src], gs_sem.at[0], gr_sem.at[src])
    load_c.wait()

    group_rows = rows_v[...].reshape(rows, width)
    tile = min(256, cols)
    for j in range(cols // tile):
        at = slice(j * tile, (j + 1) * tile)
        scores[:, at] = (
            lax.dot_general(
                group_rows, cent_v[at, :], (((1,), (1,)), ((), ())), preferred_element_type=jnp.float32
            )
            * scale
        )

    step_rows = 64
    lane = lax.broadcasted_iota(jnp.int32, (step_rows, LANES), 1)

    def combine(slots, r, n):
        peak = slots[r, 0, 0:1, :]
        for k in range(1, n):
            peak = jnp.maximum(peak, slots[r, k, 0:1, :])
        total = jnp.zeros_like(peak)
        for k in range(n):
            total = total + slots[r, k, 1:2, :] * jnp.exp(slots[r, k, 0:1, :] - peak)
        return peak + jnp.log(total)

    def row_round(r, col_potential):
        @pl.loop(0, rows // step_rows)
        def _(i):
            at = pl.ds(pl.multiple_of(i * step_rows, step_rows), step_rows)
            x = scores[at, :]
            if col_potential is not None:
                x = x + col_potential
            m = jnp.max(x, axis=1, keepdims=True)
            s = jnp.sum(jnp.exp(x - m), axis=1, keepdims=True)
            tbuf[at, :] = jnp.where(lane == 0, m, s)

        row_slots[r, c, :, :] = tbuf[...].T[0:2, :]
        for k in range(1, nc):
            push(row_slots.at[r, c], row_slots.at[r, c], rs_sem.at[r, k], rr_sem.at[r, c], (d, lax.rem(c + k, nc)))
        for k in range(1, nc):
            src = lax.rem(c + nc - k, nc)
            arrive(row_slots.at[r, src], rs_sem.at[r, k], rr_sem.at[r, src])
        row_potential = -combine(row_slots, r, nc)
        rp_v[...] = jnp.broadcast_to(row_potential, (LANES, rows)).T

    def col_round(r):
        for j in range(cols // LANES):
            at = slice(j * LANES, (j + 1) * LANES)
            x = scores[:, at] + rp_v[...]
            m = jnp.max(x, axis=0, keepdims=True)
            s = jnp.sum(jnp.exp(x - m), axis=0, keepdims=True)
            col_slots[r, d, 0:1, at] = m
            col_slots[r, d, 1:2, at] = s
        for k in range(1, nd):
            push(col_slots.at[r, d], col_slots.at[r, d], cs_sem.at[r, k], cr_sem.at[r, d], (lax.rem(d + k, nd), c))
        for k in range(1, nd):
            src = lax.rem(d + nd - k, nd)
            arrive(col_slots.at[r, src], cs_sem.at[r, k], cr_sem.at[r, src])
        return log_column - combine(col_slots, r, nd)

    col_potential = None
    for r in range(ITERS):
        row_round(r, col_potential)
        col_potential = col_round(r)
    row_round(ITERS, col_potential)

    for j in range(cols // LANES):
        at = slice(j * LANES, (j + 1) * LANES)
        w = jnp.exp(scores[:, at] + rp_v[...] + col_potential[:, at])
        mass_slots[d, :, at] = jnp.sum(w, axis=0, keepdims=True)
        assign_v[:, at] = (w * total_cols).astype(jnp.bfloat16)
    assign_copy = pltpu.make_async_copy(assign_v, assign_out, out_sem.at[0])
    assign_copy.start()
    for k in range(1, nd):
        push(mass_slots.at[d], mass_slots.at[d], ms_sem.at[k], mr_sem.at[d], (lax.rem(d + k, nd), c))

    def partial(q):
        r3 = rows_v[:, :, pl.ds(pl.multiple_of(q * feats, feats), feats)].reshape(rows, feats)
        return lax.dot_general(
            assign_v[...], r3, (((0,), (0,)), ((), ())), preferred_element_type=jnp.float32
        ).astype(jnp.bfloat16)

    for k in reversed(range(1, nd)):
        q = lax.rem(d + k, nd)
        part_send[k, :, :] = partial(q)
        push(part_send.at[k], part_recv.at[d], ps_sem.at[k], pr_sem.at[d], (q, c))
    part_recv[d, :, :] = partial(d)

    for k in range(1, nd):
        src = lax.rem(d + nd - k, nd)
        arrive(mass_slots.at[src], ms_sem.at[k], mr_sem.at[src])
    raw_mass = mass_slots[0]
    for k in range(1, nd):
        raw_mass = raw_mass + mass_slots[k]
    mass_out[...] = raw_mass * total_cols / total_rows
    mass_col = jnp.broadcast_to(raw_mass, (LANES, cols)).T

    for k in range(1, nd):
        src = lax.rem(d + nd - k, nd)
        arrive(part_recv.at[src], ps_sem.at[k], pr_sem.at[src])
    for j in range(feats // LANES):
        at = slice(j * LANES, (j + 1) * LANES)
        sums = part_recv[0, :, at].astype(jnp.float32)
        for k in range(1, nd):
            sums = sums + part_recv[k, :, at].astype(jnp.float32)
        newc_v[:, at] = sums / total_cols / mass_col
    newc_copy = pltpu.make_async_copy(newc_v, newc_out, out_sem.at[1])
    newc_copy.start()
    for copy in sends:
        copy.wait_send()
    assign_copy.wait()
    newc_copy.wait()


def wide_kernel(
    nd, nc, p_ref, c_ref, assign_out, mass_out, newc_out,
    rows_v, cent_v, scores, rp_v, tbuf, row_slots, col_slots, peak_v, mass_slots, assign_v, sums_v, newc_v,
    load_sem, gs_sem, gr_sem, ds_sem, dr_sem, rs_sem, rr_sem, cs_sem, cr_sem, out_sem,
):
    d = lax.axis_index("doc")
    c = lax.axis_index("cen")
    block, width = p_ref.shape
    cols = c_ref.shape[0]
    rows = nc * block
    feats = width // nd
    total_cols = cols * nc
    total_rows = rows * nd
    scale = 1.0 / math.sqrt(width)
    log_column = math.log(total_rows / total_cols)
    sends = []

    load_p = pltpu.make_async_copy(p_ref, rows_v.at[d, c], load_sem.at[0])
    load_c = pltpu.make_async_copy(c_ref, cent_v, load_sem.at[1])
    load_p.start()
    load_c.start()

    barrier = pltpu.get_barrier_semaphore()
    for k in range(1, nc):
        pl.semaphore_signal(barrier, inc=1, device_id=(d, lax.rem(c + k, nc)), device_id_type=MESH)
    for k in range(1, nd):
        pl.semaphore_signal(barrier, inc=1, device_id=(lax.rem(d + k, nd), c), device_id_type=MESH)
    pl.semaphore_wait(barrier, nc + nd - 2)
    load_p.wait()

    def push(src, dst, send, recv, where):
        copy = pltpu.make_async_remote_copy(
            src_ref=src, dst_ref=dst, send_sem=send, recv_sem=recv, device_id=where, device_id_type=MESH
        )
        copy.start()
        sends.append(copy)

    def arrive(ref, send, recv):
        pltpu.make_async_remote_copy(
            src_ref=ref, dst_ref=ref, send_sem=send, recv_sem=recv, device_id=(d, c), device_id_type=MESH
        ).wait_recv()

    mate = c + 1 - 2 * lax.rem(c, 2)
    half = nc // 2

    def to_docs(b, slot):
        for k in range(1, nd):
            push(rows_v.at[d, b], rows_v.at[d, b], ds_sem.at[k, slot], dr_sem.at[d, b], (lax.rem(d + k, nd), c))

    own = rows_v.at[d, c]
    for k in range(1, half):
        push(own, own, gs_sem.at[k], gr_sem.at[c], (d, lax.rem(c + 2 * k, nc)))
    push(own, own, gs_sem.at[0], gr_sem.at[c], (d, mate))
    to_docs(c, 0)
    order = [k for pair in zip(range(1, half), reversed(range(1, half))) for k in pair][: half - 1]
    for k in order:
        src = lax.rem(c + nc - 2 * k, nc)
        got = rows_v.at[d, src]
        arrive(got, gs_sem.at[half + k], gr_sem.at[src])
        push(got, got, gs_sem.at[half + k], gr_sem.at[src], (d, mate))
        to_docs(src, k)
    arrive(rows_v.at[d, mate], gs_sem.at[0], gr_sem.at[mate])
    for k in range(1, half):
        src = lax.rem(mate + nc - 2 * k, nc)
        arrive(rows_v.at[d, src], gs_sem.at[0], gr_sem.at[src])
    load_c.wait()

    def relay():
        for k in range(half):
            b = lax.rem(c + nc - 2 * k, nc)
            for q in range(1, nd):
                src = lax.rem(d + nd - q, nd)
                got = rows_v.at[src, b]
                arrive(got, ds_sem.at[0, k], dr_sem.at[src, b])
                push(got, got, ds_sem.at[nd + q, k], dr_sem.at[src, b], (d, mate))

    def arrive_doc(dd):
        for k in range(half):
            b = lax.rem(mate + nc - 2 * k, nc)
            arrive(rows_v.at[dd, b], ds_sem.at[0, k], dr_sem.at[dd, b])

    tile = min(256, cols)

    def score(dd):
        for j in range(cols // tile):
            at = slice(j * tile, (j + 1) * tile)
            scores[dd, :, at] = (
                lax.dot_general(
                    rows_v[dd].reshape(rows, width),
                    cent_v[at, :],
                    (((1,), (1,)), ((), ())),
                    preferred_element_type=jnp.float32,
                )
                * scale
            )

    score(d)

    step_rows = 64
    lane = lax.broadcasted_iota(jnp.int32, (step_rows, LANES), 1)

    def combine(slots, r, n):
        peak = slots[r, 0, 0:1, :]
        for k in range(1, n):
            peak = jnp.maximum(peak, slots[r, k, 0:1, :])
        total = jnp.zeros_like(peak)
        for k in range(n):
            total = total + slots[r, k, 1:2, :] * jnp.exp(slots[r, k, 0:1, :] - peak)
        return peak + jnp.log(total)

    def row_pass(dd, r, col_potential, keep):
        @pl.loop(0, rows // step_rows)
        def _(i):
            at = pl.ds(pl.multiple_of(i * step_rows, step_rows), step_rows)
            x = scores[dd, at, :]
            if col_potential is not None:
                x = x + col_potential
            m = jnp.max(x, axis=1, keepdims=True)
            e = jnp.exp(x - m)
            s = jnp.sum(e, axis=1, keepdims=True)
            tbuf[at, :] = jnp.where(lane == 0, m, s)
            if keep:
                scores[dd, at, :] = e
                peak_v[dd, at, :] = jnp.broadcast_to(m, (step_rows, LANES))

        row_slots[r, c, :, :] = tbuf[...].T[0:2, :]
        for k in range(1, nc):
            push(row_slots.at[r, c], row_slots.at[r, c], rs_sem.at[r, k], rr_sem.at[r, c], (d, lax.rem(c + k, nc)))

    def row_finish(r):
        for k in range(1, nc):
            src = lax.rem(c + nc - k, nc)
            arrive(row_slots.at[r, src], rs_sem.at[r, k], rr_sem.at[r, src])
        row_potential = -combine(row_slots, r, nc)
        return jnp.broadcast_to(row_potential, (LANES, rows)).T

    def col_round(r, meanwhile):
        for j in range(cols // LANES):
            at = slice(j * LANES, (j + 1) * LANES)
            x = scores[d, :, at] + rp_v[...]
            m = jnp.max(x, axis=0, keepdims=True)
            s = jnp.sum(jnp.exp(x - m), axis=0, keepdims=True)
            col_slots[r, d, 0:1, at] = m
            col_slots[r, d, 1:2, at] = s
        for k in range(1, nd):
            push(col_slots.at[r, d], col_slots.at[r, d], cs_sem.at[r, k], cr_sem.at[r, d], (lax.rem(d + k, nd), c))
        meanwhile()
        for k in range(1, nd):
            src = lax.rem(d + nd - k, nd)
            arrive(col_slots.at[r, src], cs_sem.at[r, k], cr_sem.at[r, src])
        return log_column - combine(col_slots, r, nd)

    def score_other(q):
        dd = lax.rem(d + q, nd)
        arrive_doc(dd)
        score(dd)

    work = [lambda: None, lambda: None, relay] + [functools.partial(score_other, q) for q in range(1, nd)]
    work += [lambda: None] * (2 * ITERS - len(work))
    col_potential = None
    for r in range(ITERS):
        row_pass(d, r, col_potential, False)
        work[2 * r]()
        rp_v[...] = row_finish(r)
        col_potential = col_round(r, work[2 * r + 1])
    for extra in work[2 * ITERS :]:
        extra()

    for q in range(nd):
        row_pass(lax.rem(d + q, nd), ITERS + q, col_potential, True)
    assign_copy = pltpu.make_async_copy(assign_v.at[d], assign_out, out_sem.at[0])
    my_feats = pl.ds(pl.multiple_of(d * feats, feats), feats)
    for q in range(nd):
        dd = lax.rem(d + q, nd)
        rp_v[...] = jnp.exp(peak_v[dd] + row_finish(ITERS + q))
        for j in range(cols // LANES):
            at = slice(j * LANES, (j + 1) * LANES)
            w = scores[dd, :, at] * rp_v[...]
            mass_slots[dd, :, at] = jnp.sum(w, axis=0, keepdims=True)
            assign_v[dd, :, at] = (w * total_cols).astype(jnp.bfloat16)
        if not q:
            assign_copy.start()
        part = lax.dot_general(
            rows_v[dd, :, :, my_feats].reshape(rows, feats),
            assign_v[dd],
            (((0,), (0,)), ((), ())),
            preferred_element_type=jnp.float32,
        ).astype(jnp.bfloat16).astype(jnp.float32)
        sums_v[...] = sums_v[...] + part if q else part

    raw_mass = mass_slots[0]
    for k in range(1, nd):
        raw_mass = raw_mass + mass_slots[k]
    mass_out[...] = raw_mass * total_cols / total_rows
    for j in range(cols // LANES):
        at = slice(j * LANES, (j + 1) * LANES)
        newc_v[at, :] = (sums_v[:, at] / total_cols / raw_mass[:, at]).T
    newc_copy = pltpu.make_async_copy(newc_v, newc_out, out_sem.at[1])
    newc_copy.start()
    for copy in sends:
        copy.wait_send()
    assign_copy.wait()
    newc_copy.wait()


def shards(nd, nc, passages, centroids):
    block, width = passages.shape
    cols = centroids.shape[0]
    rows = nc * block
    feats = width // nd
    any_spec = pl.BlockSpec(memory_space=pl.ANY)
    dma = pltpu.SemaphoreType.DMA
    f32, bf16 = jnp.float32, jnp.bfloat16
    wide = nd * rows * cols <= 2**22 and nc % 2 == 0
    if wide:
        body = wide_kernel
        limit = 52 * 1024 * 1024
        scratch = [
            pltpu.VMEM((nd, nc, block, width), bf16),
            pltpu.VMEM((cols, width), bf16),
            pltpu.VMEM((nd, rows, cols), f32),
            pltpu.VMEM((rows, LANES), f32),
            pltpu.VMEM((rows, LANES), f32),
            pltpu.VMEM((ITERS + nd, nc, 2, rows), f32),
            pltpu.VMEM((ITERS, nd, 2, cols), f32),
            pltpu.VMEM((nd, rows, LANES), f32),
            pltpu.VMEM((nd, 1, cols), f32),
            pltpu.VMEM((nd, rows, cols), bf16),
            pltpu.VMEM((feats, cols), f32),
            pltpu.VMEM((cols, feats), f32),
            dma((2,)),
            dma((nc,)),
            dma((nc,)),
            dma((2 * nd, nc // 2)),
            dma((nd, nc)),
            dma((ITERS + nd, nc)),
            dma((ITERS + nd, nc)),
            dma((ITERS, nd)),
            dma((ITERS, nd)),
            dma((2,)),
        ]
    else:
        body = kernel
        limit = 52 * 1024 * 1024
        scratch = [
            pltpu.VMEM((nc, block, width), bf16),
            pltpu.VMEM((cols, width), bf16),
            pltpu.VMEM((rows, cols), f32),
            pltpu.VMEM((rows, LANES), f32),
            pltpu.VMEM((rows, LANES), f32),
            pltpu.VMEM((ITERS + 1, nc, 2, rows), f32),
            pltpu.VMEM((ITERS, nd, 2, cols), f32),
            pltpu.VMEM((nd, 1, cols), f32),
            pltpu.VMEM((rows, cols), bf16),
            pltpu.VMEM((nd, cols, feats), bf16),
            pltpu.VMEM((nd, cols, feats), bf16),
            pltpu.VMEM((cols, feats), f32),
            dma((2,)),
            dma((nc,)),
            dma((nc,)),
            dma((ITERS + 1, nc)),
            dma((ITERS + 1, nc)),
            dma((ITERS, nd)),
            dma((ITERS, nd)),
            dma((nd,)),
            dma((nd,)),
            dma((nd,)),
            dma((nd,)),
            dma((2,)),
        ]
    assign, masses, newc = pl.pallas_call(
        functools.partial(body, nd, nc),
        out_shape=(
            jax.ShapeDtypeStruct((rows, cols), bf16),
            jax.ShapeDtypeStruct((1, cols), f32),
            jax.ShapeDtypeStruct((cols, feats), f32),
        ),
        in_specs=[pl.BlockSpec(memory_space=pltpu.MemorySpace.HBM)] * 2,
        out_specs=(any_spec, pl.BlockSpec(memory_space=pltpu.VMEM), any_spec),
        scratch_shapes=scratch,
        compiler_params=pltpu.CompilerParams(
            collective_id=0, has_side_effects=True, vmem_limit_bytes=limit
        ),
    )(passages, centroids)
    return assign, masses.reshape(cols), newc


def solution(mesh):
    nd, nc = mesh.shape["doc"], mesh.shape["cen"]
    in_specs = (P(("doc", "cen"), None), P("cen", None))
    out_specs = (P("doc", "cen"), P("cen"), P("cen", "doc"))
    return jax.shard_map(
        functools.partial(shards, nd, nc), mesh=mesh, in_specs=in_specs, out_specs=out_specs, check_vma=False
    )
```
